32 devices in a mesh: dp: 16 (over z, y, core), tensor: 2 (over x).
Axes of the slice: x: 2, y: 2, z: 4, core: 2. Of those that a mesh axis runs over, the one named last changes fastest.
Arguments:
- tokens: bfloat16 [4096, 768], P(('dp', 'tensor')), may hold values from -6 to 6
- segments: int32 [4096], P('dp'), may hold values from 0 to 4095, as said below
- positions: int32 [4096], P('dp'), may hold values from 0 to 255, as said below
- cotangent: bfloat16 [4096, 768], P(('dp', 'tensor')), may hold values from -6 to 6
- qkv_weight: bfloat16 [1, 768, 2304], P(None, 'dp', 'tensor'), may hold values from -1 to 1
- qkv_bias: bfloat16 [1, 2304], P(None, ('tensor', 'dp')), may hold values from -3 to 3
- out_weight: bfloat16 [1, 768, 768], P(None, 'tensor', 'dp'), may hold values from -0.625 to 0.625
- out_bias: bfloat16 [1, 768], P(None, 'dp'), may hold values from -3 to 3
- up_weight: bfloat16 [1, 768, 3072], P(None, 'dp', 'tensor'), may hold values from -0.21875 to 0.21875
- up_bias: bfloat16 [1, 3072], P(None, ('tensor', 'dp')), may hold values from -3 to 3
- down_weight: bfloat16 [1, 3072, 768], P(None, 'tensor', 'dp'), may hold values from -0.109375 to 0.109375
- down_bias: bfloat16 [1, 768], P(None, 'dp'), may hold values from -3 to 3
- norm1_gain: bfloat16 [1, 768], P(None, 'dp'), may hold values from 0.5 to 1.5
- norm1_bias: bfloat16 [1, 768], P(None, 'dp'), may hold values from -2 to 2
- norm2_gain: bfloat16 [1, 768], P(None, 'dp'), may hold values from 0.5 to 1.5
- norm2_bias: bfloat16 [1, 768], P(None, 'dp'), may hold values from -2 to 2
Outputs:
- hidden_out: bfloat16 [1, 4096, 768], P(None, ('dp', 'tensor'))
- input_grad: float32 [4096, 768], P(('dp', 'tensor'))
- grad_qkv_weight: float32 [1, 768, 2304], P(None, 'dp', 'tensor')
- grad_qkv_bias: float32 [1, 2304], P(None, ('tensor', 'dp'))
- grad_out_weight: float32 [1, 768, 768], P(None, 'tensor', 'dp')
- grad_out_bias: float32 [1, 768], P(None, 'dp')
- grad_up_weight: float32 [1, 768, 3072], P(None, 'dp', 'tensor')
- grad_up_bias: float32 [1, 3072], P(None, ('tensor', 'dp'))
- grad_down_weight: float32 [1, 3072, 768], P(None, 'tensor', 'dp')
- grad_down_bias: float32 [1, 768], P(None, 'dp')
- grad_norm1_gain: float32 [1, 768], P(None, 'dp')
- grad_norm1_bias: float32 [1, 768], P(None, 'dp')
- grad_norm2_gain: float32 [1, 768], P(None, 'dp')
- grad_norm2_bias: float32 [1, 768], P(None, 'dp')
The draws below stay inside these ranges and needn't reach their ends.
Inputs may be any that keep to these rules, and one draw needn't show every extreme that they name: `segments`: segment numbers never fall along the array, a new segment begins at the first token of every sequence of 256 tokens, and the last token of the array forms a segment of its own. `positions`: A token's position is its distance to the first token of its segment.
All inputs are finite; a program needn't handle non-finite values.
Results may differ from the reference program's by a relative error of at most 0.0094.
Values may be sent and summed in bfloat16 or wider, within the bound.
A program may use at most 128 MiB of HBM per device.

```python
import jax
import jax.numpy as jnp
from jax import lax

D = 768
HEADS = 12
HEAD = 64
ROT = 16
FF = 3072
LAYERS = 1
SEQ = 256
TOKENS = 4096


def segment_plan(key):
    coin_draw = jax.random.randint(jax.random.fold_in(key, 11), (TOKENS,), 0, 48)
    slot_index = jnp.arange(TOKENS, dtype=jnp.int32)
    starts = (coin_draw == 0) & (slot_index >= SEQ) | (slot_index % SEQ == 0) | (slot_index == TOKENS - 1)
    first_slot = lax.cummax(jnp.where(starts, slot_index, 0), axis=0)
    return (first_slot.astype(jnp.int32), (slot_index - first_slot).astype(jnp.int32))


def draw_segments(key, part):
    return segment_plan(key)[0]


def draw_positions(key, part):
    return segment_plan(key)[1]


def draw_qkv_weight(key, part):
    return (jnp.clip(jax.random.normal(key, (LAYERS, D, 3 * D), jnp.float32), -6.0, 6.0) * D ** (-0.5)).astype(jnp.bfloat16)


def raised(array, stream_key, source, target, shards_of, factor):
    def block_of(axis_at):
        return (jnp.arange(array.shape[axis_at]) // (array.shape[axis_at] // shards_of)).reshape((-1,) + (1,) * (array.ndim - 1 - axis_at))

    one_side = jax.random.permutation(stream_key, shards_of)[block_of(target)]
    far = (block_of(target) + shards_of // 2) % shards_of
    return jnp.where((block_of(source) == one_side) | (block_of(source) == far), factor * array, array)


def steps_of(rng, shape, split, least, largest):
    def one(axis_at, parts):
        heights = jax.random.uniform(jax.random.fold_in(jax.random.fold_in(rng, 6), axis_at), (parts,), jnp.float32, least / len(split), largest / len(split))
        return jnp.repeat(jnp.exp(heights), shape[axis_at] // parts).reshape((-1,) + (1,) * (len(shape) - axis_at - 1))

    factor_of = one(*split[0])
    for cut in split[1:]:
        factor_of = factor_of * one(*cut)
    return factor_of


def centred(own_key, dims, deviation, most, split=(), kind=jnp.bfloat16):
    values = jax.random.normal(own_key, dims, jnp.float32) * deviation
    if len(split) > 0:
        values = steps_of(own_key, dims, split, -0.22, 0.18) * values
    return jnp.clip(values, min=-most, max=most).astype(kind)


def heavy_noise(stream_key, dims, deviation, most, shards, heavy, held_as=jnp.bfloat16):
    entries = deviation * jax.random.normal(stream_key, dims, jnp.float32)
    if shards:
        entries = entries * steps_of(stream_key, dims, shards, -0.22, 0.18)
    return jnp.clip(raised(entries, jax.random.fold_in(stream_key, 3), *heavy), -most, most).astype(held_as)


def setup_inputs(seed: int = 0) -> dict:
    seeds = jax.random.split(jax.random.key(seed), 17)
    return {
        "tokens": centred(seeds[0], (TOKENS, D), 1.0, 6.0, ((0, 32),)),
        "segments": draw_segments(jax.random.fold_in(seeds[16], 71), 0),
        "positions": draw_positions(jax.random.fold_in(seeds[16], 71), 0),
        "cotangent": heavy_noise(seeds[3], (TOKENS, D), 1.0, 6.0, ((0, 32),), (0, 1, 32, 2.75)),
        "qkv_weight": draw_qkv_weight(jax.random.fold_in(seeds[16], 71), 0),
        "qkv_bias": centred(seeds[5], (LAYERS, 3 * D), 0.5, 3.0, ((1, 32),)),
        "out_weight": centred(seeds[6], (LAYERS, D, D), (D // 8) ** -0.5, 0.625, ((1, 2), (2, 16))),
        "out_bias": centred(seeds[7], (LAYERS, D), 0.5, 3.0, ((1, 16),)),
        "up_weight": centred(seeds[8], (LAYERS, D, FF), D ** -0.5, 0.21875, ((1, 16), (2, 2))),
        "up_bias": centred(seeds[9], (LAYERS, FF), 0.5, 3.0, ((1, 32),)),
        "down_weight": centred(seeds[10], (LAYERS, FF, D), FF ** -0.5, 0.109375, ((1, 2), (2, 16))),
        "down_bias": centred(seeds[11], (LAYERS, D), 0.5, 3.0, ((1, 16),)),
        "norm1_gain": jnp.clip(1.0 + 0.1 * jax.random.normal(seeds[12], (LAYERS, D), jnp.float32), 0.5, 1.5).astype(jnp.bfloat16),
        "norm1_bias": centred(seeds[13], (LAYERS, D), 0.3, 2.0, ((1, 16),)),
        "norm2_gain": jnp.clip(1.0 + 0.1 * jax.random.normal(seeds[14], (LAYERS, D), jnp.float32), 0.5, 1.5).astype(jnp.bfloat16),
        "norm2_bias": centred(seeds[15], (LAYERS, D), 0.3, 2.0, ((1, 16),)),
    }


EPS = 1e-05

def rotary_tables(pos_ids):
    half_rot = ROT // 2
    freq_index = jnp.arange(half_rot, dtype=jnp.float32)
    inverse = jnp.power(jnp.float32(10000.0), -2.0 * freq_index / ROT)
    angles = pos_ids.astype(jnp.float32)[:, None] * inverse[None, :]
    cos_tab = jnp.concatenate([jnp.cos(angles), jnp.cos(angles)], axis=1)
    sin_tab = jnp.concatenate([jnp.sin(angles), jnp.sin(angles)], axis=1)
    return (cos_tab, sin_tab)

def rotate(values, cos_tab, sin_tab):
    half_rot = ROT // 2
    rotary = values[..., :ROT]
    turned = jnp.concatenate([-rotary[..., half_rot:], rotary[..., :half_rot]], axis=-1)
    rotated = rotary * cos_tab[:, None, :] + turned * sin_tab[:, None, :]
    return jnp.concatenate([rotated, values[..., ROT:]], axis=-1)

def unrotate(grad_vals, cos_tab, sin_tab):
    half_rot = ROT // 2
    rotary = grad_vals[..., :ROT]
    scaled = rotary * sin_tab[:, None, :]
    back_part = jnp.concatenate([scaled[..., half_rot:], -scaled[..., :half_rot]], axis=-1)
    return jnp.concatenate([rotary * cos_tab[:, None, :] + back_part, grad_vals[..., ROT:]], axis=-1)

def layernorm(values, gain_row, bias_row):
    centre = values - lax.optimization_barrier(jnp.mean(values, axis=-1, keepdims=True))
    inv_std = lax.rsqrt(lax.optimization_barrier(jnp.mean(centre * centre, axis=-1, keepdims=True)) + EPS)
    normed = centre * inv_std
    return (normed * gain_row + bias_row, normed, inv_std)

def norm_back(upstream, normed, inv_std, gain_row):
    scaled = upstream * gain_row
    mean_term = lax.optimization_barrier(jnp.mean(scaled, axis=-1, keepdims=True))
    proj_term = lax.optimization_barrier(jnp.mean(scaled * normed, axis=-1, keepdims=True))
    grad_in = inv_std * (scaled - mean_term - normed * proj_term)
    return (grad_in, lax.optimization_barrier(jnp.sum(upstream * normed, axis=0)), lax.optimization_barrier(jnp.sum(upstream, axis=0)))

def gelu_slope(hidden_pre):
    cumul_part = 0.5 * (1.0 + jax.scipy.special.erf(hidden_pre * 0.7071067811865476))
    return cumul_part + hidden_pre * jnp.exp(-0.5 * hidden_pre * hidden_pre) * 0.3989422804014327

def seq_mask(seg_ids):
    slot_index = jnp.arange(seg_ids.shape[0])
    return (slot_index[None, :] <= slot_index[:, None]) & (seg_ids[None, :] == seg_ids[:, None])

def attention_scores(query_rot, key_rot, allowed):
    scores = jnp.einsum('qhd,khd->hqk', query_rot.astype(jnp.float32), key_rot.astype(jnp.float32)) * HEAD ** (-0.5)
    return jnp.where(allowed[None], scores, -jnp.inf)

def layer_forward(rows_in, allowed, cos_tab, sin_tab, params):
    qkv_w, qkv_b, out_w, out_b, up_w, up_b, down_w, down_b, gain_one, bias_one, gain_two, bias_two = params
    seq_len = rows_in.shape[0]
    residual = rows_in.astype(jnp.float32)
    normed_one, unit_one, inv_one = layernorm(residual, gain_one.astype(jnp.float32), bias_one.astype(jnp.float32))
    normed_two, unit_two, inv_two = layernorm(residual, gain_two.astype(jnp.float32), bias_two.astype(jnp.float32))
    normed_one = normed_one.astype(jnp.bfloat16)
    normed_two = normed_two.astype(jnp.bfloat16)
    projected = jnp.dot(normed_one, qkv_w, preferred_element_type=jnp.float32) + qkv_b.astype(jnp.float32)
    projected = projected.reshape(seq_len, HEADS, 3, HEAD)
    query_rot = rotate(projected[:, :, 0], cos_tab, sin_tab).astype(jnp.bfloat16)
    key_rot = rotate(projected[:, :, 1], cos_tab, sin_tab).astype(jnp.bfloat16)
    value_rows = projected[:, :, 2].astype(jnp.bfloat16)
    scores = attention_scores(query_rot, key_rot, allowed)
    row_peak = lax.optimization_barrier(jnp.max(scores, axis=-1, keepdims=True))
    row_total = lax.optimization_barrier(jnp.sum(jnp.exp(scores - row_peak), axis=-1, keepdims=True))
    log_total = row_peak + jnp.log(row_total)
    weights_bf = jnp.exp(scores - log_total).astype(jnp.bfloat16)
    attended = jnp.einsum('hqk,khd->qhd', weights_bf.astype(jnp.float32), value_rows.astype(jnp.float32)).astype(jnp.bfloat16)
    attended_flat = attended.reshape(seq_len, D)
    hidden_pre = jnp.dot(normed_two, up_w, preferred_element_type=jnp.float32) + up_b.astype(jnp.float32)
    hidden_act = jax.nn.gelu(hidden_pre, approximate=False).astype(jnp.bfloat16)
    branches = jnp.dot(attended_flat, out_w, preferred_element_type=jnp.float32) + jnp.dot(hidden_act, down_w, preferred_element_type=jnp.float32)
    output = (residual + branches + out_b.astype(jnp.float32) + down_b.astype(jnp.float32)).astype(jnp.bfloat16)
    saved_state = (unit_one, inv_one, unit_two, inv_two, normed_one, normed_two, query_rot, key_rot, value_rows, attended, log_total, hidden_pre, hidden_act)
    return (output, saved_state)

def layer_backward(upstream, saved_state, allowed, cos_tab, sin_tab, params):
    qkv_w, qkv_b, out_w, out_b, up_w, up_b, down_w, down_b, gain_one, bias_one, gain_two, bias_two = params
    unit_one, inv_one, unit_two, inv_two, normed_one, normed_two, query_rot, key_rot, value_rows, attended, log_total, hidden_pre, hidden_act = saved_state
    seq_len = upstream.shape[0]
    upstream_bf = upstream.astype(jnp.bfloat16)
    bias_grad = lax.optimization_barrier(jnp.sum(upstream, axis=0))
    grad_down = jnp.dot(hidden_act.T, upstream_bf, preferred_element_type=jnp.float32)
    hidden_grad = (jnp.dot(upstream_bf, down_w.T, preferred_element_type=jnp.float32) * gelu_slope(hidden_pre)).astype(jnp.bfloat16)
    grad_up = jnp.dot(normed_two.T, hidden_grad, preferred_element_type=jnp.float32)
    grad_upbias = lax.optimization_barrier(jnp.sum(hidden_grad.astype(jnp.float32), axis=0))
    two_grad = jnp.dot(hidden_grad, up_w.T, preferred_element_type=jnp.float32)
    attended_flat = attended.reshape(seq_len, D)
    grad_out = jnp.dot(attended_flat.T, upstream_bf, preferred_element_type=jnp.float32)
    attended_grad = jnp.dot(upstream_bf, out_w.T, preferred_element_type=jnp.float32).astype(jnp.bfloat16).reshape(seq_len, HEADS, HEAD)
    scores = attention_scores(query_rot, key_rot, allowed)
    weights_full = jnp.where(allowed[None], jnp.exp(scores - log_total), 0.0)
    weights_bf = weights_full.astype(jnp.bfloat16)
    row_delta = jnp.einsum('qhd,qhd->hq', attended.astype(jnp.float32), attended_grad.astype(jnp.float32))
    value_grad = jnp.einsum('hqk,qhd->khd', weights_bf.astype(jnp.float32), attended_grad.astype(jnp.float32))
    weight_grad = jnp.einsum('qhd,khd->hqk', attended_grad.astype(jnp.float32), value_rows.astype(jnp.float32))
    score_grad = (weights_full * (weight_grad - row_delta[:, :, None]) * HEAD ** (-0.5)).astype(jnp.bfloat16)
    query_grad = jnp.einsum('hqk,khd->qhd', score_grad.astype(jnp.float32), key_rot.astype(jnp.float32))
    key_grad = jnp.einsum('hqk,qhd->khd', score_grad.astype(jnp.float32), query_rot.astype(jnp.float32))
    stacked = jnp.stack([unrotate(query_grad, cos_tab, sin_tab), unrotate(key_grad, cos_tab, sin_tab), value_grad], axis=2)
    stacked = stacked.reshape(seq_len, 3 * D).astype(jnp.bfloat16)
    grad_qkv = jnp.dot(normed_one.T, stacked, preferred_element_type=jnp.float32)
    grad_qkvbias = lax.optimization_barrier(jnp.sum(stacked.astype(jnp.float32), axis=0))
    one_grad = jnp.dot(stacked, qkv_w.T, preferred_element_type=jnp.float32)
    in_one, gain_one_grad, bias_one_grad = norm_back(one_grad, unit_one, inv_one, gain_one.astype(jnp.float32))
    in_two, gain_two_grad, bias_two_grad = norm_back(two_grad, unit_two, inv_two, gain_two.astype(jnp.float32))
    rows_grad = upstream + in_one + in_two
    return (rows_grad, (grad_qkv, grad_qkvbias, grad_out, bias_grad, grad_up, grad_upbias, grad_down, gain_one_grad, bias_one_grad, gain_two_grad, bias_two_grad))

def reference(tokens, segments, positions, cotangent, qkv_weight, qkv_bias, out_weight, out_bias, up_weight, up_bias, down_weight, down_bias, norm1_gain, norm1_bias, norm2_gain, norm2_bias):
    sources = (qkv_weight, qkv_bias, out_weight, out_bias, up_weight, up_bias, down_weight, down_bias, norm1_gain, norm1_bias, norm2_gain, norm2_bias)
    param_sets = [tuple((source[layer_idx] for source in sources)) for layer_idx in range(LAYERS)]
    seq_count = tokens.shape[0] // SEQ

    def one_sequence(carry_acc, inputs):
        seq_rows, seg_ids, pos_ids, cot_rows = inputs
        cos_tab, sin_tab = rotary_tables(pos_ids)
        allowed = seq_mask(seg_ids)
        outputs = []
        saves = []
        current = seq_rows
        for layer_idx in range(LAYERS):
            current, saved_state = layer_forward(current, allowed, cos_tab, sin_tab, param_sets[layer_idx])
            outputs.append(current)
            saves.append(saved_state)
        upstream = cot_rows.astype(jnp.float32)
        new_carry = list(carry_acc)
        for layer_idx in reversed(range(LAYERS)):
            upstream, layer_grads = layer_backward(upstream, saves[layer_idx], allowed, cos_tab, sin_tab, param_sets[layer_idx])
            new_carry[layer_idx] = tuple((old_sum + new_term for old_sum, new_term in zip(carry_acc[layer_idx], layer_grads)))
        return (tuple(new_carry), (jnp.stack(outputs), upstream))
    grad_shapes = ((D, 3 * D), (3 * D,), (D, D), (D,), (D, FF), (FF,), (FF, D), (D,), (D,), (D,), (D,))
    zero_grads = tuple((tuple((jnp.zeros(shape_item, jnp.float32) for shape_item in grad_shapes)) for layer_idx in range(LAYERS)))
    final_acc, (hidden_seq, grad_seq) = lax.scan(one_sequence, zero_grads, (tokens.reshape(seq_count, SEQ, D), segments.reshape(seq_count, SEQ), positions.reshape(seq_count, SEQ), cotangent.reshape(seq_count, SEQ, D)))
    hidden_out = jnp.transpose(hidden_seq, (1, 0, 2, 3)).reshape(LAYERS, seq_count * SEQ, D)
    input_grad = grad_seq.reshape(seq_count * SEQ, D)

    def stacked_grad(member):
        return jnp.stack([final_acc[layer_idx][member] for layer_idx in range(LAYERS)])
    return (hidden_out, input_grad, stacked_grad(0), stacked_grad(1), stacked_grad(2), stacked_grad(3), stacked_grad(4), stacked_grad(5), stacked_grad(6), stacked_grad(3), stacked_grad(7), stacked_grad(8), stacked_grad(9), stacked_grad(10))
```

```python
import functools

import jax
import jax.numpy as jnp
from jax import lax
from jax.experimental import pallas as pl
from jax.experimental.pallas import tpu as pltpu
from jax.sharding import PartitionSpec as P

HEAD = 64
ROT = 16
EPS = 1e-05
F32 = jnp.float32
BF16 = jnp.bfloat16
VMEM = pltpu.VMEM


def up128(n):
    return -(-n // 128) * 128


class Sizes:
    def __init__(self, rows, up_q, qkv_q, out_q, qkvb, upb):
        self.rows, self.up_q, self.qkv_q, self.out_q = rows, up_q, qkv_q, out_q
        self.qkvb, self.upb = qkvb, upb
        self.qb_cols, self.ub_cols = -(-qkvb // rows), -(-upb // rows)
        self.down = up_q
        self.qkv = 2 * up_q
        self.small = self.qkv + qkv_q
        self.n_small = 6 + self.qb_cols + self.ub_cols
        self.out = up128(self.small + self.n_small)
        self.cols = up128(self.out + out_q)
        self.tile = self.small // 128 * 128
        self.tile_end = self.out

    def pack(self, up, down, qkv, small, out):
        lead = up.shape[:-1]
        gap = self.out - self.small - small.shape[-1]
        tail = self.cols - self.out - self.out_q
        parts = [up, down, qkv, small, jnp.zeros(lead + (gap,), BF16), out]
        if tail:
            parts.append(jnp.zeros(lead + (tail,), BF16))
        return jnp.concatenate([p.astype(BF16) for p in parts], axis=-1)


def places(n_outer):
    dp = lax.axis_index("dp")
    x = lax.axis_index("tensor")
    core = lax.rem(dp, 2)
    chip = dp // 2
    inner = lax.rem(chip, 2)
    outer = chip // 2
    return dp, x, core, chip, inner, outer


def dev(chip, core, x):
    return {"dp": chip * 2 + core, "tensor": x}


def greet(partners, outer, n_outer, up, down):
    barrier = pltpu.get_barrier_semaphore()

    def tell(partner):
        pl.semaphore_signal(
            barrier, inc=1, device_id=partner, device_id_type=pl.DeviceIdType.MESH
        )

    for partner in partners:
        tell(partner)
    pl.when(outer < n_outer - 1)(lambda: tell(up))
    pl.when(outer > 0)(lambda: tell(down))
    chained = jnp.minimum(outer, 1) + jnp.minimum(n_outer - 1 - outer, 1)
    pl.semaphore_wait(barrier, len(partners) + chained)


def rcopy(src, dst, send, recv, where):
    return pltpu.make_async_remote_copy(
        src_ref=src,
        dst_ref=dst,
        send_sem=send,
        recv_sem=recv,
        device_id=where,
        device_id_type=pl.DeviceIdType.MESH,
    )


def partner_list(n_outer):
    dp, x, core, chip, inner, outer = places(n_outer)
    sibling = dev(chip, 1 - core, x)
    across = dev(chip, core, 1 - x)
    diagonal = dev(chip, 1 - core, 1 - x)
    inner_peer = dev(outer * 2 + 1 - inner, core, x)
    up = dev((outer + 1) * 2 + inner, core, x)
    down = dev((outer - 1) * 2 + inner, core, x)
    return sibling, across, diagonal, inner_peer, up, down


def gather_kernel(
    n_outer, p_ref, a_ref, w_ref, t_ref, loc_sem, grp_s, grp_r, sib_s, sib_r, ch_s, ch_r, in_s, in_r
):
    dp, x, core, chip, inner, outer = places(n_outer)
    sibling, across, diagonal, inner_peer, up, down = partner_list(n_outer)
    own_w = pltpu.make_async_copy(p_ref.at[core], w_ref.at[chip, core], loc_sem.at[0])
    own_t = pltpu.make_async_copy(a_ref, t_ref.at[core, x], loc_sem.at[1])
    own_w.start()
    own_t.start()
    greet([sibling, across, diagonal, inner_peer], outer, n_outer, up, down)
    sib = rcopy(p_ref.at[1 - core], w_ref.at[chip, core], sib_s, sib_r, sibling)
    sib.start()
    own_w.wait()
    sib.wait_recv()
    last = n_outer - 1

    def chain(way, step):
        block = outer - step if way == 0 else outer + step
        there = (outer < last) & (block >= 0) if way == 0 else (outer > 0) & (block <= last)
        spot = w_ref.at[block * 2 + inner]
        where = up if way == 0 else down
        return there, lambda: rcopy(spot, spot, ch_s.at[way, step], ch_r.at[way, step], where)

    def arrival(way, step):
        block = outer - 1 - step if way == 0 else outer + 1 + step
        there = block >= 0 if way == 0 else block <= last
        spot = w_ref.at[block * 2 + inner]
        return there, lambda: rcopy(spot, spot, ch_s.at[way, step], ch_r.at[way, step], up)

    def forward(way, step, mine):
        block = outer - 1 - step if way == 0 else outer + 1 + step
        there = block >= 0 if way == 0 else block <= last
        spot = w_ref.at[block * 2 + (inner if mine else 1 - inner)]
        return there, lambda: rcopy(spot, spot, in_s.at[way, step], in_r.at[way, step], inner_peer)

    def act(pair, what):
        there, copy = pair
        pl.when(there)(lambda: what(copy()))

    def start(copy):
        copy.start()

    for way in range(2):
        act(chain(way, 0), start)
    own = w_ref.at[chip]
    mine = rcopy(own, own, in_s.at[0, last], in_r.at[0, last], inner_peer)
    mine.start()
    group = []
    for slot, where in enumerate((sibling, across, diagonal)):
        copy = rcopy(a_ref, t_ref.at[core, x], grp_s.at[slot], grp_r.at[slot], where)
        copy.start()
        group.append(copy)
    for step in range(last):
        for way in range(2):
            act(arrival(way, step), lambda copy: copy.wait_recv())
            if step + 1 < last:
                act(chain(way, step + 1), start)
            act(forward(way, step, True), start)
    for copy in group:
        copy.wait_recv()
    mine.wait_recv()
    for step in range(last):
        for way in range(2):
            act(forward(way, step, False), lambda copy: copy.wait_recv())
    own_t.wait()
    sib.wait_send()
    mine.wait_send()
    for copy in group:
        copy.wait_send()
    for step in range(last):
        for way in range(2):
            act(chain(way, step), lambda copy: copy.wait_send())
            act(forward(way, step, True), lambda copy: copy.wait_send())


def scatter_kernel(
    sizes,
    n_outer,
    n2t_ref,
    cott_ref,
    n1t_ref,
    du_ref,
    act_ref,
    dqkv_ref,
    att_ref,
    small_ref,
    h_ref,
    r_ref,
    hs_ref,
    x_ref,
    first_buf,
    b1,
    send_buf,
    cbuf,
    acc,
    hr,
    small_out,
    small_in,
    grp_s,
    grp_r,
    in_s,
    in_r,
    ch_s,
    ch_r,
    sib_s,
    sib_r,
    sm_s,
    sm_r,
):
    dp, x, core, chip, inner, outer = places(n_outer)
    sibling, across, diagonal, inner_peer, up, down = partner_list(n_outer)
    last = n_outer - 1
    rows = sizes.rows
    lo, hi = sizes.tile, sizes.tile_end

    def block(target, put):
        def product(left, right):
            if rows % 16 == 0:
                lhs = left[target].reshape(2 * rows, -1)
                out = jnp.dot(lhs, right[...], preferred_element_type=F32)
                return out.reshape(2, rows, -1)
            return jnp.stack(
                [
                    jnp.dot(left[target, side], right[...], preferred_element_type=F32)
                    for side in range(2)
                ]
            )

        put(0, sizes.down, product(n2t_ref, du_ref))
        put(sizes.down, sizes.qkv, product(cott_ref, act_ref))
        part = product(n1t_ref, dqkv_ref)
        cut = lo - sizes.qkv
        put(sizes.qkv, lo, part[:, :, :cut])
        put(lo, hi, part[:, :, cut:] + small_ref[target])
        put(sizes.out, sizes.cols, product(cott_ref, att_ref))

    def to_acc(start, stop, value):
        acc[:, :, start:stop] = value

    greet([sibling, across, diagonal, inner_peer], outer, n_outer, up, down)
    group = []
    spots = ((sibling, 1 - core, x), (across, core, 1 - x), (diagonal, 1 - core, 1 - x))
    for slot, (where, to_core, to_x) in enumerate(spots):
        copy = rcopy(h_ref.at[to_core, to_x], hr.at[slot], grp_s.at[slot], grp_r.at[slot], where)
        copy.start()
        group.append(copy)

    def in_order(what):
        @pl.loop(0, last)
        def _(tick):
            back = last - tick
            pl.when(outer <= tick)(lambda: what(0, outer + back))
            pl.when(outer >= back)(lambda: what(1, outer - back))

    def exchange(target):
        return rcopy(
            first_buf.at[target], b1.at[target], in_s.at[target], in_r.at[target], inner_peer
        )

    def passing(way, target):
        return rcopy(
            send_buf.at[target],
            cbuf.at[way, target],
            ch_s.at[way, target],
            ch_r.at[way, target],
            up if way == 0 else down,
        )

    def send_first(target):
        def put(start, stop, value):
            first_buf[target, :, :, start:stop] = value.astype(BF16)

        block(target * 2 + 1 - inner, put)
        exchange(target).start()

    def send_second(way, target):
        block(target * 2 + inner, to_acc)
        exchange(target).wait_recv()
        acc[...] += b1[target].astype(F32)
        started = outer > 0 if way == 0 else outer < last

        @pl.when(started)
        def _():
            passing(way, target).wait_recv()
            acc[...] += cbuf[way, target].astype(F32)

        send_buf[target] = acc[...].astype(BF16)
        passing(way, target).start()

    in_order(lambda way, target: send_first(target))
    send_first(outer)
    in_order(send_second)
    for copy in group:
        copy.wait_recv()
    hs_ref[...] = (
        h_ref[core, x].astype(F32)
        + hr[0].astype(F32)
        + hr[1].astype(F32)
        + hr[2].astype(F32)
    )
    block(chip, to_acc)
    exchange(outer).wait_recv()
    acc[...] += b1[outer].astype(F32)
    for way in range(2):

        @pl.when(outer > 0 if way == 0 else outer < last)
        def _():
            passing(way, outer).wait_recv()
            acc[...] += cbuf[way, outer].astype(F32)

    sib = rcopy(acc.at[1 - core], r_ref.at[core], sib_s, sib_r, sibling)
    sib.start()
    r_ref[core] = acc[core]
    sib.wait_recv()
    small_out[...] = r_ref[0, :, lo:hi] + r_ref[1, :, lo:hi]
    small = rcopy(small_out, small_in, sm_s, sm_r, across)
    small.start()
    small.wait_recv()
    x_ref[0] = small_out[...]
    x_ref[1] = small_out[...] + small_in[...]
    sib.wait_send()
    small.wait_send()
    for copy in group:
        copy.wait_send()
    exchange(outer).wait_send()

    def sent(way, target):
        exchange(target).wait_send()
        passing(way, target).wait_send()

    in_order(sent)


def gather(sizes, n_outer, packed, rows):
    dma = pltpu.SemaphoreType.DMA
    full = pl.BlockSpec(memory_space=VMEM)
    return pl.pallas_call(
        functools.partial(gather_kernel, n_outer),
        out_shape=(
            jax.ShapeDtypeStruct((2 * n_outer, 2) + packed.shape[1:], BF16),
            jax.ShapeDtypeStruct((2, 2) + rows.shape, BF16),
        ),
        in_specs=[full, full],
        out_specs=(full, full),
        scratch_shapes=[
            dma((2,)),
            dma((3,)),
            dma((3,)),
            dma,
            dma,
            dma((2, n_outer)),
            dma((2, n_outer)),
            dma((2, n_outer)),
            dma((2, n_outer)),
        ],
        compiler_params=pltpu.CompilerParams(
            collective_id=0, has_side_effects=True, vmem_limit_bytes=60 * 2**20
        ),
        name="gather",
    )(packed, rows)


def scatter(sizes, n_outer, operands, parts):
    dma = pltpu.SemaphoreType.DMA
    full = pl.BlockSpec(memory_space=VMEM)
    block = (2, sizes.rows, sizes.cols)
    width = sizes.tile_end - sizes.tile
    return pl.pallas_call(
        functools.partial(scatter_kernel, sizes, n_outer),
        out_shape=(
            jax.ShapeDtypeStruct(block, F32),
            jax.ShapeDtypeStruct(parts.shape[2:], F32),
            jax.ShapeDtypeStruct((2, sizes.rows, width), F32),
        ),
        in_specs=[full] * (len(operands) + 1),
        out_specs=(full, full, full),
        scratch_shapes=[
            VMEM((n_outer,) + block, BF16),
            VMEM((n_outer,) + block, BF16),
            VMEM((n_outer,) + block, BF16),
            VMEM((2, n_outer) + block, BF16),
            VMEM(block, F32),
            VMEM((3,) + parts.shape[2:], BF16),
            VMEM((sizes.rows, width), F32),
            VMEM((sizes.rows, width), F32),
            dma((3,)),
            dma((3,)),
            dma((n_outer,)),
            dma((n_outer,)),
            dma((2, n_outer)),
            dma((2, n_outer)),
            dma,
            dma,
            dma,
            dma,
        ],
        compiler_params=pltpu.CompilerParams(
            collective_id=1, has_side_effects=True, vmem_limit_bytes=60 * 2**20
        ),
        name="scatter",
    )(*operands, parts)


def rotary_tables(pos_ids):
    half_rot = ROT // 2
    freq_index = jnp.arange(half_rot, dtype=F32)
    inverse = jnp.power(F32(10000.0), -2.0 * freq_index / ROT)
    angles = pos_ids[..., None] * inverse
    cos_tab = jnp.concatenate([jnp.cos(angles), jnp.cos(angles)], axis=-1)
    sin_tab = jnp.concatenate([jnp.sin(angles), jnp.sin(angles)], axis=-1)
    return (cos_tab[:, None], sin_tab[:, None])


def rotate(values, cos_tab, sin_tab):
    half_rot = ROT // 2
    rotary = values[..., :ROT]
    turned = jnp.concatenate([-rotary[..., half_rot:], rotary[..., :half_rot]], axis=-1)
    return jnp.concatenate([rotary * cos_tab + turned * sin_tab, values[..., ROT:]], axis=-1)


def unrotate(grad_vals, cos_tab, sin_tab):
    half_rot = ROT // 2
    rotary = grad_vals[..., :ROT]
    scaled = rotary * sin_tab
    back_part = jnp.concatenate([scaled[..., half_rot:], -scaled[..., :half_rot]], axis=-1)
    return jnp.concatenate([rotary * cos_tab + back_part, grad_vals[..., ROT:]], axis=-1)


def unit_rows(values):
    centre = values - jnp.mean(values, axis=-1, keepdims=True)
    inv_std = lax.rsqrt(jnp.mean(centre * centre, axis=-1, keepdims=True) + EPS)
    return centre * inv_std, inv_std


def dot(a, b, ca, cb):
    return lax.dot_general(a, b, (((ca,), (cb,)), ((), ())), preferred_element_type=F32)


def fold(vector, count, rows, cols):
    per = vector.shape[0] // count
    padded = jnp.pad(vector.reshape(count, per), ((0, 0), (0, rows * cols - per)))
    return padded.reshape(count, rows, cols)


def on_device(
    tokens,
    segments,
    positions,
    cotangent,
    qkv_weight,
    qkv_bias,
    out_weight,
    out_bias,
    up_weight,
    up_bias,
    down_weight,
    down_bias,
    norm1_gain,
    norm1_bias,
    norm2_gain,
    norm2_bias,
):
    dp_size = lax.axis_size("dp")
    n_outer = dp_size // 4
    core = lax.rem(lax.axis_index("dp"), 2)
    x = lax.axis_index("tensor")
    own, width = tokens.shape
    rows = qkv_weight.shape[1]
    seq_len = segments.shape[0]
    qkv_q, up_q, out_q = (
        qkv_weight.shape[2] // 2,
        up_weight.shape[2] // 2,
        out_weight.shape[1] // 2,
    )
    sizes = Sizes(rows, up_q, qkv_q, out_q, qkv_bias.shape[1], up_bias.shape[1])
    heads = out_q // HEAD

    def halves(w):
        return jnp.swapaxes(w.reshape(rows, 2, -1), 0, 1)

    def halves_t(w):
        return jnp.swapaxes(w.reshape(2, -1, rows), 1, 2)

    small = jnp.concatenate(
        [
            jnp.stack(
                [
                    norm1_gain[0],
                    norm1_bias[0],
                    norm2_gain[0],
                    norm2_bias[0],
                    out_bias[0],
                    down_bias[0],
                ],
                axis=1,
            ),
            fold(qkv_bias[0], 1, rows, sizes.qb_cols)[0],
            fold(up_bias[0], 1, rows, sizes.ub_cols)[0],
        ],
        axis=1,
    )
    packed = sizes.pack(
        halves(up_weight[0]),
        halves_t(down_weight[0]),
        halves(qkv_weight[0]),
        jnp.broadcast_to(small[None], (2,) + small.shape),
        halves_t(out_weight[0]),
    )
    own_pos = lax.dynamic_slice_in_dim(positions, x * own, own, 0).astype(BF16)
    rows_in = jnp.concatenate(
        [tokens, cotangent, jnp.pad(own_pos[:, None], ((0, 0), (0, 127)))], axis=1
    )
    gathered, group_rows = gather(sizes, n_outer, packed, rows_in)

    flat = gathered.reshape(dp_size * rows, sizes.cols)
    up_w = flat[:, :up_q]
    down_wt = flat[:, up_q : 2 * up_q]
    qkv_w = flat[:, sizes.qkv : sizes.qkv + qkv_q]
    out_wt = flat[:, sizes.out : sizes.out + out_q]
    smalls = flat[:, sizes.small : sizes.small + sizes.n_small].astype(F32)
    vecs = smalls[:, :6].T
    by_dev = smalls.reshape(dp_size, rows, sizes.n_small)
    qb = by_dev[:, :, 6 : 6 + sizes.qb_cols].reshape(dp_size, -1)[:, : sizes.qkvb].reshape(-1)
    ub = by_dev[:, :, 6 + sizes.qb_cols :].reshape(dp_size, -1)[:, : sizes.upb].reshape(-1)
    qkv_b = lax.dynamic_slice_in_dim(qb, core * qkv_q, qkv_q, 0)
    up_b = lax.dynamic_slice_in_dim(ub, core * up_q, up_q, 0)

    group_rows = group_rows.reshape(4 * own, -1)
    count = 4 * own
    seqs = count // seq_len
    xs = group_rows[:, :width].astype(F32)
    cot = group_rows[:, width : 2 * width]
    pos = group_rows[:, 2 * width].astype(F32).reshape(seqs, seq_len)
    cos_tab, sin_tab = rotary_tables(pos)
    query_index = jnp.arange(seq_len, dtype=F32)
    key_index = query_index[None, None, :]
    first_key = query_index[None, :] - pos
    allowed = (
        (key_index <= query_index[None, :, None]) & (key_index >= first_key[:, :, None])
    )[:, None]

    unit, _ = unit_rows(xs)
    n1 = (unit * vecs[0] + vecs[1]).astype(BF16)
    n2 = (unit * vecs[2] + vecs[3]).astype(BF16)
    projected = (dot(n1, qkv_w, 1, 0) + qkv_b).reshape(seqs, seq_len, heads, 3, HEAD)
    projected = jnp.transpose(projected, (3, 0, 2, 1, 4))
    query = rotate(projected[0], cos_tab, sin_tab).astype(BF16)
    key = rotate(projected[1], cos_tab, sin_tab).astype(BF16)
    value = projected[2].astype(BF16)
    scale = HEAD ** (-0.5)

    def ein(spec, a, b):
        return jnp.einsum(spec, a, b, preferred_element_type=F32)

    scores = jnp.where(allowed, ein("shqd,shkd->shqk", query, key) * scale, -jnp.inf)
    peak = jnp.max(scores, axis=-1, keepdims=True)
    log_total = peak + jnp.log(jnp.sum(jnp.exp(scores - peak), axis=-1, keepdims=True))
    weights = jnp.exp(scores - log_total)
    weights_bf = weights.astype(BF16)
    attended = ein("shqk,shkd->shqd", weights_bf, value).astype(BF16)
    attended_flat = jnp.swapaxes(attended, 1, 2).reshape(count, out_q)
    pre = dot(n2, up_w, 1, 0) + up_b
    cumul = 0.5 * (1.0 + jax.scipy.special.erf(pre * 0.7071067811865476))
    act = (pre * cumul).astype(BF16)
    slope = cumul + pre * jnp.exp(-0.5 * pre * pre) * 0.3989422804014327
    mixed = dot(attended_flat, out_wt, 1, 1) + dot(act, down_wt, 1, 1)

    du = (dot(cot, down_wt, 1, 0) * slope).astype(BF16)
    g_upb = jnp.sum(du.astype(F32), axis=0)
    dn2 = dot(du, up_w, 1, 1)
    d_att = dot(cot, out_wt, 1, 0).astype(BF16).reshape(seqs, seq_len, heads, HEAD)
    d_att = jnp.swapaxes(d_att, 1, 2)
    delta = jnp.sum(attended.astype(F32) * d_att.astype(F32), axis=-1, keepdims=True)
    d_value = ein("shqk,shqd->shkd", weights_bf, d_att)
    d_weight = ein("shqd,shkd->shqk", d_att, value)
    d_score = (weights * (d_weight - delta) * scale).astype(BF16)
    d_query = unrotate(ein("shqk,shkd->shqd", d_score, key), cos_tab, sin_tab)
    d_key = unrotate(ein("shqk,shqd->shkd", d_score, query), cos_tab, sin_tab)
    d_qkv = jnp.stack([d_query, d_key, d_value], axis=0).astype(BF16)
    d_qkv = jnp.transpose(d_qkv, (1, 3, 2, 0, 4)).reshape(count, qkv_q)
    g_qkvb = jnp.sum(d_qkv.astype(F32), axis=0)
    dn1 = dot(d_qkv, qkv_w, 1, 1)
    back = dn1 * vecs[0] + dn2 * vecs[2]
    up_rows = cotangent.astype(F32)
    norm_rows = jnp.stack(
        [
            jnp.sum(dn1 * unit, axis=0),
            jnp.sum(dn1, axis=0),
            jnp.sum(dn2 * unit, axis=0),
            jnp.sum(dn2, axis=0),
            jnp.sum(up_rows, axis=0),
            jnp.zeros((width,), F32),
        ],
        axis=1,
    ).reshape(dp_size, rows, 6)
    own_half = jnp.arange(2)[:, None] == core
    qb_full = jnp.where(own_half, g_qkvb[None], 0.0).reshape(-1)
    ub_full = jnp.where(own_half, g_upb[None], 0.0).reshape(-1)
    small_grads = jnp.concatenate(
        [
            norm_rows,
            fold(qb_full, dp_size, rows, sizes.qb_cols),
            fold(ub_full, dp_size, rows, sizes.ub_cols),
        ],
        axis=2,
    )
    small_grads = jnp.pad(
        small_grads,
        (
            (0, 0),
            (0, 0),
            (sizes.small - sizes.tile, sizes.tile_end - sizes.small - sizes.n_small),
        ),
    ).reshape(dp_size // 2, 2, rows, -1)

    def turned(values):
        return values.T.reshape(dp_size // 2, 2, rows, count)

    operands = (
        turned(n2),
        turned(cot),
        turned(n1),
        du,
        act,
        jnp.pad(d_qkv, ((0, 0), (0, sizes.out - sizes.small))),
        jnp.pad(attended_flat, ((0, 0), (0, sizes.cols - sizes.out - out_q))),
        small_grads,
    )
    parts = jnp.concatenate([mixed.astype(BF16), back.astype(BF16)], axis=1)
    parts = parts.reshape(2, 2, own, 2 * width)
    reduced, sums, small_sum = scatter(sizes, n_outer, operands, parts)

    own_x = tokens.astype(F32)
    own_unit, own_inv = unit_rows(own_x)
    hidden = (own_x + sums[:, :width] + vecs[4] + vecs[5]).astype(BF16)
    total = sums[:, width:]
    mean_term = jnp.mean(total, axis=-1, keepdims=True)
    proj_term = jnp.mean(total * own_unit, axis=-1, keepdims=True)
    input_grad = up_rows + own_inv * (total - mean_term - own_unit * proj_term)

    def columns(start, size):
        return jnp.swapaxes(reduced[:, :, start : start + size], 0, 1).reshape(rows, 2 * size)

    def columns_t(start, size):
        return jnp.swapaxes(reduced[:, :, start : start + size], 1, 2).reshape(2 * size, rows)

    off = sizes.small - sizes.tile
    fin = small_sum[1, :, off : off + 6].T
    qb_out = small_sum[0, :, off + 6 : off + 6 + sizes.qb_cols].reshape(-1)[: sizes.qkvb]
    ub_at = off + 6 + sizes.qb_cols
    ub_out = small_sum[0, :, ub_at : ub_at + sizes.ub_cols].reshape(-1)[: sizes.upb]
    return (
        hidden[None],
        input_grad,
        columns(sizes.qkv, qkv_q)[None],
        qb_out[None],
        columns_t(sizes.out, out_q)[None],
        fin[4][None],
        columns(0, up_q)[None],
        ub_out[None],
        columns_t(sizes.down, up_q)[None],
        fin[4][None],
        fin[0][None],
        fin[1][None],
        fin[2][None],
        fin[3][None],
    )


def solution(mesh):
    in_specs = (
        P(("dp", "tensor"), None),
        P("dp"),
        P("dp"),
        P(("dp", "tensor"), None),
        P(None, "dp", "tensor"),
        P(None, ("tensor", "dp")),
        P(None, "tensor", "dp"),
        P(None, "dp"),
        P(None, "dp", "tensor"),
        P(None, ("tensor", "dp")),
        P(None, "tensor", "dp"),
        P(None, "dp"),
        P(None, "dp"),
        P(None, "dp"),
        P(None, "dp"),
        P(None, "dp"),
    )
    out_specs = (
        P(None, ("dp", "tensor"), None),
        P(("dp", "tensor"), None),
        P(None, "dp", "tensor"),
        P(None, ("tensor", "dp")),
        P(None, "tensor", "dp"),
        P(None, "dp"),
        P(None, "dp", "tensor"),
        P(None, ("tensor", "dp")),
        P(None, "tensor", "dp"),
        P(None, "dp"),
        P(None, "dp"),
        P(None, "dp"),
        P(None, "dp"),
        P(None, "dp"),
    )
    return jax.shard_map(
        on_device, mesh=mesh, in_specs=in_specs, out_specs=out_specs, check_vma=False
    )
```

```python
import functools

import jax
import jax.numpy as jnp
from jax import lax
from jax.experimental import pallas as pl
from jax.experimental.pallas import tpu as pltpu
from jax.sharding import PartitionSpec as P

HEAD = 64
ROT = 16
EPS = 1e-05
F32 = jnp.float32
BF16 = jnp.bfloat16
VMEM = pltpu.VMEM


def up128(n):
    return -(-n // 128) * 128


class Sizes:
    def __init__(self, rows, up_q, qkv_q, out_q, qkvb, upb):
        self.rows, self.up_q, self.qkv_q, self.out_q = rows, up_q, qkv_q, out_q
        self.qkvb, self.upb = qkvb, upb
        self.qb_cols, self.ub_cols = -(-qkvb // rows), -(-upb // rows)
        self.down = up_q
        self.qkv = 2 * up_q
        self.small = self.qkv + qkv_q
        self.n_small = 6 + self.qb_cols + self.ub_cols
        self.out = up128(self.small + self.n_small)
        self.cols = up128(self.out + out_q)
        self.tile = self.small // 128 * 128
        self.tile_end = self.out

    def pack(self, up, down, qkv, small, out):
        lead = up.shape[:-1]
        gap = self.out - self.small - small.shape[-1]
        tail = self.cols - self.out - self.out_q
        parts = [up, down, qkv, small, jnp.zeros(lead + (gap,), BF16), out]
        if tail:
            parts.append(jnp.zeros(lead + (tail,), BF16))
        return jnp.concatenate([p.astype(BF16) for p in parts], axis=-1)


def places(n_outer):
    dp = lax.axis_index("dp")
    x = lax.axis_index("tensor")
    core = lax.rem(dp, 2)
    chip = dp // 2
    inner = lax.rem(chip, 2)
    outer = chip // 2
    return dp, x, core, chip, inner, outer


def dev(chip, core, x):
    return {"dp": chip * 2 + core, "tensor": x}


def greet(partners, outer, n_outer, up, down):
    barrier = pltpu.get_barrier_semaphore()

    def tell(partner):
        pl.semaphore_signal(
            barrier, inc=1, device_id=partner, device_id_type=pl.DeviceIdType.MESH
        )

    for partner in partners:
        tell(partner)
    pl.when(outer < n_outer - 1)(lambda: tell(up))
    pl.when(outer > 0)(lambda: tell(down))
    chained = jnp.minimum(outer, 1) + jnp.minimum(n_outer - 1 - outer, 1)
    pl.semaphore_wait(barrier, len(partners) + chained)


def rcopy(src, dst, send, recv, where):
    return pltpu.make_async_remote_copy(
        src_ref=src,
        dst_ref=dst,
        send_sem=send,
        recv_sem=recv,
        device_id=where,
        device_id_type=pl.DeviceIdType.MESH,
    )


def partner_list(n_outer):
    dp, x, core, chip, inner, outer = places(n_outer)
    sibling = dev(chip, 1 - core, x)
    across = dev(chip, core, 1 - x)
    diagonal = dev(chip, 1 - core, 1 - x)
    inner_peer = dev(outer * 2 + 1 - inner, core, x)
    up = dev((outer + 1) * 2 + inner, core, x)
    down = dev((outer - 1) * 2 + inner, core, x)
    return sibling, across, diagonal, inner_peer, up, down


def gather_kernel(
    n_outer, p_ref, a_ref, w_ref, t_ref, loc_sem, grp_s, grp_r, sib_s, sib_r, ch_s, ch_r, in_s, in_r
):
    dp, x, core, chip, inner, outer = places(n_outer)
    sibling, across, diagonal, inner_peer, up, down = partner_list(n_outer)
    own_w = pltpu.make_async_copy(p_ref.at[core], w_ref.at[chip, core], loc_sem.at[0])
    own_t = pltpu.make_async_copy(a_ref, t_ref.at[core, x], loc_sem.at[1])
    own_w.start()
    own_t.start()
    greet([sibling, across, diagonal, inner_peer], outer, n_outer, up, down)
    sib = rcopy(p_ref.at[1 - core], w_ref.at[chip, core], sib_s, sib_r, sibling)
    sib.start()
    own_w.wait()
    sib.wait_recv()
    last = n_outer - 1

    def chain(way, step):
        block = outer - step if way == 0 else outer + step
        there = (outer < last) & (block >= 0) if way == 0 else (outer > 0) & (block <= last)
        spot = w_ref.at[block * 2 + inner]
        where = up if way == 0 else down
        return there, lambda: rcopy(spot, spot, ch_s.at[way, step], ch_r.at[way, step], where)

    def arrival(way, step):
        block = outer - 1 - step if way == 0 else outer + 1 + step
        there = block >= 0 if way == 0 else block <= last
        spot = w_ref.at[block * 2 + inner]
        return there, lambda: rcopy(spot, spot, ch_s.at[way, step], ch_r.at[way, step], up)

    def forward(way, step, mine):
        block = outer - 1 - step if way == 0 else outer + 1 + step
        there = block >= 0 if way == 0 else block <= last
        spot = w_ref.at[block * 2 + (inner if mine else 1 - inner)]
        return there, lambda: rcopy(spot, spot, in_s.at[way, step], in_r.at[way, step], inner_peer)

    def act(pair, what):
        there, copy = pair
        pl.when(there)(lambda: what(copy()))

    def start(copy):
        copy.start()

    for way in range(2):
        act(chain(way, 0), start)
    own = w_ref.at[chip]
    mine = rcopy(own, own, in_s.at[0, last], in_r.at[0, last], inner_peer)
    mine.start()
    group = []
    for slot, where in enumerate((sibling, across, diagonal)):
        copy = rcopy(a_ref, t_ref.at[core, x], grp_s.at[slot], grp_r.at[slot], where)
        copy.start()
        group.append(copy)
    for step in range(last):
        for way in range(2):
            act(arrival(way, step), lambda copy: copy.wait_recv())
            if step + 1 < last:
                act(chain(way, step + 1), start)
            act(forward(way, step, True), start)
    for copy in group:
        copy.wait_recv()
    mine.wait_recv()
    for step in range(last):
        for way in range(2):
            act(forward(way, step, False), lambda copy: copy.wait_recv())
    own_t.wait()
    sib.wait_send()
    mine.wait_send()
    for copy in group:
        copy.wait_send()
    for step in range(last):
        for way in range(2):
            act(chain(way, step), lambda copy: copy.wait_send())
            act(forward(way, step, True), lambda copy: copy.wait_send())


def scatter_kernel(
    sizes,
    n_outer,
    n2t_ref,
    cott_ref,
    n1t_ref,
    du_ref,
    act_ref,
    dqkv_ref,
    att_ref,
    small_ref,
    h_ref,
    d_ref,
    r_ref,
    hs_ref,
    ds_ref,
    x_ref,
    first_buf,
    b1,
    send_buf,
    cbuf,
    acc,
    hr,
    small_out,
    small_in,
    grp_s,
    grp_r,
    in_s,
    in_r,
    ch_s,
    ch_r,
    sib_s,
    sib_r,
    sm_s,
    sm_r,
):
    dp, x, core, chip, inner, outer = places(n_outer)
    sibling, across, diagonal, inner_peer, up, down = partner_list(n_outer)
    last = n_outer - 1
    rows = sizes.rows
    lo, hi = sizes.tile, sizes.tile_end

    def block(target, put):
        def product(left, right):
            if rows % 16 == 0:
                lhs = left[target].reshape(2 * rows, -1)
                out = jnp.dot(lhs, right[...], preferred_element_type=F32)
                return out.reshape(2, rows, -1)
            return jnp.stack(
                [
                    jnp.dot(left[target, side], right[...], preferred_element_type=F32)
                    for side in range(2)
                ]
            )

        put(0, sizes.down, product(n2t_ref, du_ref))
        put(sizes.down, sizes.qkv, product(cott_ref, act_ref))
        part = product(n1t_ref, dqkv_ref)
        cut = lo - sizes.qkv
        put(sizes.qkv, lo, part[:, :, :cut])
        put(lo, hi, part[:, :, cut:] + small_ref[target])
        end = sizes.out + sizes.out_q
        put(sizes.out, end, product(cott_ref, att_ref))
        if end < sizes.cols:
            put(end, sizes.cols, jnp.zeros((2, rows, sizes.cols - end), F32))

    def to_acc(start, stop, value):
        acc[:, :, start:stop] = value

    greet([sibling, across, diagonal, inner_peer], outer, n_outer, up, down)
    group = []
    spots = ((sibling, 1 - core, x), (across, core, 1 - x), (diagonal, 1 - core, 1 - x))
    for slot, (where, to_core, to_x) in enumerate(spots):
        for kind, part in enumerate((h_ref, d_ref)):
            copy = rcopy(
                part.at[to_core, to_x],
                hr.at[kind, slot],
                grp_s.at[kind, slot],
                grp_r.at[kind, slot],
                where,
            )
            copy.start()
            group.append(copy)

    def in_order(what):
        @pl.loop(0, last)
        def _(tick):
            back = last - tick
            pl.when(outer <= tick)(lambda: what(0, outer + back))
            pl.when(outer >= back)(lambda: what(1, outer - back))

    def exchange(target):
        return rcopy(
            first_buf.at[target], b1.at[target], in_s.at[target], in_r.at[target], inner_peer
        )

    def passing(way, target):
        return rcopy(
            send_buf.at[target],
            cbuf.at[way, target],
            ch_s.at[way, target],
            ch_r.at[way, target],
            up if way == 0 else down,
        )

    def send_first(target):
        def put(start, stop, value):
            first_buf[target, :, :, start:stop] = value.astype(BF16)

        block(target * 2 + 1 - inner, put)
        exchange(target).start()

    def send_second(way, target):
        block(target * 2 + inner, to_acc)
        exchange(target).wait_recv()
        acc[...] += b1[target].astype(F32)
        started = outer > 0 if way == 0 else outer < last

        @pl.when(started)
        def _():
            passing(way, target).wait_recv()
            acc[...] += cbuf[way, target].astype(F32)

        send_buf[target] = acc[...].astype(BF16)
        passing(way, target).start()

    in_order(lambda way, target: send_first(target))
    send_first(outer)
    in_order(send_second)
    for copy in group:
        copy.wait_recv()
    for kind, (part, out) in enumerate(((h_ref, hs_ref), (d_ref, ds_ref))):
        out[...] = (
            part[core, x].astype(F32)
            + hr[kind, 0].astype(F32)
            + hr[kind, 1].astype(F32)
            + hr[kind, 2].astype(F32)
        )
    block(chip, to_acc)
    exchange(outer).wait_recv()
    acc[...] += b1[outer].astype(F32)
    for way in range(2):

        @pl.when(outer > 0 if way == 0 else outer < last)
        def _():
            passing(way, outer).wait_recv()
            acc[...] += cbuf[way, outer].astype(F32)

    sib = rcopy(acc.at[1 - core], r_ref.at[core], sib_s, sib_r, sibling)
    sib.start()
    r_ref[core] = acc[core]
    sib.wait_recv()
    small_out[...] = r_ref[0, :, lo:hi] + r_ref[1, :, lo:hi]
    small = rcopy(small_out, small_in, sm_s, sm_r, across)
    small.start()
    small.wait_recv()
    x_ref[0] = small_out[...]
    x_ref[1] = small_out[...] + small_in[...]
    sib.wait_send()
    small.wait_send()
    for copy in group:
        copy.wait_send()
    exchange(outer).wait_send()

    def sent(way, target):
        exchange(target).wait_send()
        passing(way, target).wait_send()

    in_order(sent)


def gather(sizes, n_outer, packed, rows):
    dma = pltpu.SemaphoreType.DMA
    full = pl.BlockSpec(memory_space=VMEM)
    return pl.pallas_call(
        functools.partial(gather_kernel, n_outer),
        out_shape=(
            jax.ShapeDtypeStruct((2 * n_outer, 2) + packed.shape[1:], BF16),
            jax.ShapeDtypeStruct((2, 2) + rows.shape, BF16),
        ),
        in_specs=[full, full],
        out_specs=(full, full),
        scratch_shapes=[
            dma((2,)),
            dma((3,)),
            dma((3,)),
            dma,
            dma,
            dma((2, n_outer)),
            dma((2, n_outer)),
            dma((2, n_outer)),
            dma((2, n_outer)),
        ],
        compiler_params=pltpu.CompilerParams(
            collective_id=0, has_side_effects=True, vmem_limit_bytes=60 * 2**20
        ),
        name="gather",
    )(packed, rows)


def scatter(sizes, n_outer, operands, mixed, back):
    dma = pltpu.SemaphoreType.DMA
    full = pl.BlockSpec(memory_space=VMEM)
    block = (2, sizes.rows, sizes.cols)
    width = sizes.tile_end - sizes.tile
    return pl.pallas_call(
        functools.partial(scatter_kernel, sizes, n_outer),
        out_shape=(
            jax.ShapeDtypeStruct(block, F32),
            jax.ShapeDtypeStruct(mixed.shape[2:], F32),
            jax.ShapeDtypeStruct(mixed.shape[2:], F32),
            jax.ShapeDtypeStruct((2, sizes.rows, width), F32),
        ),
        in_specs=[full] * (len(operands) + 2),
        out_specs=(full, full, full, full),
        scratch_shapes=[
            VMEM((n_outer,) + block, BF16),
            VMEM((n_outer,) + block, BF16),
            VMEM((n_outer,) + block, BF16),
            VMEM((2, n_outer) + block, BF16),
            VMEM(block, F32),
            VMEM((2, 3) + mixed.shape[2:], BF16),
            VMEM((sizes.rows, width), F32),
            VMEM((sizes.rows, width), F32),
            dma((2, 3)),
            dma((2, 3)),
            dma((n_outer,)),
            dma((n_outer,)),
            dma((2, n_outer)),
            dma((2, n_outer)),
            dma,
            dma,
            dma,
            dma,
        ],
        compiler_params=pltpu.CompilerParams(
            collective_id=1, has_side_effects=True, vmem_limit_bytes=60 * 2**20
        ),
        name="scatter",
    )(*operands, mixed, back)


def rotary_tables(pos_ids):
    half_rot = ROT // 2
    freq_index = jnp.arange(half_rot, dtype=F32)
    inverse = jnp.power(F32(10000.0), -2.0 * freq_index / ROT)
    angles = pos_ids[..., None] * inverse
    cos_tab = jnp.concatenate([jnp.cos(angles), jnp.cos(angles)], axis=-1)
    sin_tab = jnp.concatenate([jnp.sin(angles), jnp.sin(angles)], axis=-1)
    return (cos_tab[:, None], sin_tab[:, None])


def rotate(values, cos_tab, sin_tab):
    half_rot = ROT // 2
    rotary = values[..., :ROT]
    turned = jnp.concatenate([-rotary[..., half_rot:], rotary[..., :half_rot]], axis=-1)
    return jnp.concatenate([rotary * cos_tab + turned * sin_tab, values[..., ROT:]], axis=-1)


def unrotate(grad_vals, cos_tab, sin_tab):
    half_rot = ROT // 2
    rotary = grad_vals[..., :ROT]
    scaled = rotary * sin_tab
    back_part = jnp.concatenate([scaled[..., half_rot:], -scaled[..., :half_rot]], axis=-1)
    return jnp.concatenate([rotary * cos_tab + back_part, grad_vals[..., ROT:]], axis=-1)


def unit_rows(values):
    centre = values - jnp.mean(values, axis=-1, keepdims=True)
    inv_std = lax.rsqrt(jnp.mean(centre * centre, axis=-1, keepdims=True) + EPS)
    return centre * inv_std, inv_std


def dot(a, b, ca, cb):
    return lax.dot_general(a, b, (((ca,), (cb,)), ((), ())), preferred_element_type=F32)


def fold(vector, count, rows, cols):
    per = vector.shape[0] // count
    padded = jnp.pad(vector.reshape(count, per), ((0, 0), (0, rows * cols - per)))
    return padded.reshape(count, rows, cols)


def on_device(
    tokens,
    segments,
    positions,
    cotangent,
    qkv_weight,
    qkv_bias,
    out_weight,
    out_bias,
    up_weight,
    up_bias,
    down_weight,
    down_bias,
    norm1_gain,
    norm1_bias,
    norm2_gain,
    norm2_bias,
):
    dp_size = lax.axis_size("dp")
    n_outer = dp_size // 4
    core = lax.rem(lax.axis_index("dp"), 2)
    x = lax.axis_index("tensor")
    own, width = tokens.shape
    rows = qkv_weight.shape[1]
    seq_len = segments.shape[0]
    qkv_q, up_q, out_q = (
        qkv_weight.shape[2] // 2,
        up_weight.shape[2] // 2,
        out_weight.shape[1] // 2,
    )
    sizes = Sizes(rows, up_q, qkv_q, out_q, qkv_bias.shape[1], up_bias.shape[1])
    heads = out_q // HEAD

    def halves(w):
        return jnp.swapaxes(w.reshape(rows, 2, -1), 0, 1)

    def halves_t(w):
        return jnp.swapaxes(w.reshape(2, -1, rows), 1, 2)

    small = jnp.concatenate(
        [
            jnp.stack(
                [
                    norm1_gain[0],
                    norm1_bias[0],
                    norm2_gain[0],
                    norm2_bias[0],
                    out_bias[0],
                    down_bias[0],
                ],
                axis=1,
            ),
            fold(qkv_bias[0], 1, rows, sizes.qb_cols)[0],
            fold(up_bias[0], 1, rows, sizes.ub_cols)[0],
        ],
        axis=1,
    )
    packed = sizes.pack(
        halves(up_weight[0]),
        halves_t(down_weight[0]),
        halves(qkv_weight[0]),
        jnp.broadcast_to(small[None], (2,) + small.shape),
        halves_t(out_weight[0]),
    )
    own_pos = lax.dynamic_slice_in_dim(positions, x * own, own, 0).astype(BF16)
    rows_in = jnp.concatenate(
        [tokens, cotangent, jnp.pad(own_pos[:, None], ((0, 0), (0, 127)))], axis=1
    )
    gathered, group_rows = gather(sizes, n_outer, packed, rows_in)

    flat = gathered.reshape(dp_size * rows, sizes.cols)
    up_w = flat[:, :up_q]
    down_wt = flat[:, up_q : 2 * up_q]
    qkv_w = flat[:, sizes.qkv : sizes.qkv + qkv_q]
    out_wt = flat[:, sizes.out : sizes.out + out_q]
    smalls = flat[:, sizes.small : sizes.small + sizes.n_small].astype(F32)
    vecs = smalls[:, :6].T
    by_dev = smalls.reshape(dp_size, rows, sizes.n_small)
    qb = by_dev[:, :, 6 : 6 + sizes.qb_cols].reshape(dp_size, -1)[:, : sizes.qkvb].reshape(-1)
    ub = by_dev[:, :, 6 + sizes.qb_cols :].reshape(dp_size, -1)[:, : sizes.upb].reshape(-1)
    qkv_b = lax.dynamic_slice_in_dim(qb, core * qkv_q, qkv_q, 0)
    up_b = lax.dynamic_slice_in_dim(ub, core * up_q, up_q, 0)

    group_rows = group_rows.reshape(4 * own, -1)
    count = 4 * own
    seqs = count // seq_len
    xs = group_rows[:, :width].astype(F32)
    cot = group_rows[:, width : 2 * width]
    pos = group_rows[:, 2 * width].astype(F32).reshape(seqs, seq_len)
    cos_tab, sin_tab = rotary_tables(pos)
    query_index = jnp.arange(seq_len, dtype=F32)
    key_index = query_index[None, None, :]
    first_key = query_index[None, :] - pos
    allowed = (
        (key_index <= query_index[None, :, None]) & (key_index >= first_key[:, :, None])
    )[:, None]

    unit, _ = unit_rows(xs)
    n1 = (unit * vecs[0] + vecs[1]).astype(BF16)
    n2 = (unit * vecs[2] + vecs[3]).astype(BF16)
    projected = (dot(n1, qkv_w, 1, 0) + qkv_b).reshape(seqs, seq_len, heads, 3, HEAD)
    projected = jnp.transpose(projected, (3, 0, 2, 1, 4))
    query = rotate(projected[0], cos_tab, sin_tab).astype(BF16)
    key = rotate(projected[1], cos_tab, sin_tab).astype(BF16)
    value = projected[2].astype(BF16)
    scale = HEAD ** (-0.5)

    def ein(spec, a, b):
        return jnp.einsum(spec, a, b, preferred_element_type=F32)

    scores = jnp.where(allowed, ein("shqd,shkd->shqk", query, key) * scale, -jnp.inf)
    peak = jnp.max(scores, axis=-1, keepdims=True)
    log_total = peak + jnp.log(jnp.sum(jnp.exp(scores - peak), axis=-1, keepdims=True))
    weights = jnp.exp(scores - log_total)
    weights_bf = weights.astype(BF16)
    attended = ein("shqk,shkd->shqd", weights_bf, value).astype(BF16)
    attended_flat = jnp.swapaxes(attended, 1, 2).reshape(count, out_q)
    pre = dot(n2, up_w, 1, 0) + up_b
    cumul = 0.5 * (1.0 + jax.scipy.special.erf(pre * 0.7071067811865476))
    act = (pre * cumul).astype(BF16)
    slope = cumul + pre * jnp.exp(-0.5 * pre * pre) * 0.3989422804014327
    mixed = dot(attended_flat, out_wt, 1, 1) + dot(act, down_wt, 1, 1)

    du = (dot(cot, down_wt, 1, 0) * slope).astype(BF16)
    g_upb = jnp.sum(du.astype(F32), axis=0)
    dn2 = dot(du, up_w, 1, 1)
    d_att = dot(cot, out_wt, 1, 0).astype(BF16).reshape(seqs, seq_len, heads, HEAD)
    d_att = jnp.swapaxes(d_att, 1, 2)
    delta = jnp.sum(attended.astype(F32) * d_att.astype(F32), axis=-1, keepdims=True)
    d_value = ein("shqk,shqd->shkd", weights_bf, d_att)
    d_weight = ein("shqd,shkd->shqk", d_att, value)
    d_score = (weights * (d_weight - delta) * scale).astype(BF16)
    d_query = unrotate(ein("shqk,shkd->shqd", d_score, key), cos_tab, sin_tab)
    d_key = unrotate(ein("shqk,shqd->shkd", d_score, query), cos_tab, sin_tab)
    d_qkv = jnp.stack([d_query, d_key, d_value], axis=0).astype(BF16)
    d_qkv = jnp.transpose(d_qkv, (1, 3, 2, 0, 4)).reshape(count, qkv_q)
    g_qkvb = jnp.sum(d_qkv.astype(F32), axis=0)
    dn1 = dot(d_qkv, qkv_w, 1, 1)
    back = dn1 * vecs[0] + dn2 * vecs[2]
    up_rows = cotangent.astype(F32)
    norm_rows = jnp.stack(
        [
            jnp.sum(dn1 * unit, axis=0),
            jnp.sum(dn1, axis=0),
            jnp.sum(dn2 * unit, axis=0),
            jnp.sum(dn2, axis=0),
            jnp.sum(up_rows, axis=0),
            jnp.zeros((width,), F32),
        ],
        axis=1,
    ).reshape(dp_size, rows, 6)
    own_half = jnp.arange(2)[:, None] == core
    qb_full = jnp.where(own_half, g_qkvb[None], 0.0).reshape(-1)
    ub_full = jnp.where(own_half, g_upb[None], 0.0).reshape(-1)
    small_grads = jnp.concatenate(
        [
            norm_rows,
            fold(qb_full, dp_size, rows, sizes.qb_cols),
            fold(ub_full, dp_size, rows, sizes.ub_cols),
        ],
        axis=2,
    )
    small_grads = jnp.pad(
        small_grads,
        (
            (0, 0),
            (0, 0),
            (sizes.small - sizes.tile, sizes.tile_end - sizes.small - sizes.n_small),
        ),
    ).reshape(dp_size // 2, 2, rows, -1)

    def turned(values):
        return values.T.reshape(dp_size // 2, 2, rows, count)

    operands = (
        turned(n2),
        turned(cot),
        turned(n1),
        du,
        act,
        jnp.pad(d_qkv, ((0, 0), (0, sizes.out - sizes.small))),
        attended_flat,
        small_grads,
    )
    reduced, mixed_sum, total, small_sum = scatter(
        sizes,
        n_outer,
        operands,
        mixed.astype(BF16).reshape(2, 2, own, width),
        back.astype(BF16).reshape(2, 2, own, width),
    )

    own_x = tokens.astype(F32)
    own_unit, own_inv = unit_rows(own_x)
    hidden = (own_x + mixed_sum + vecs[4] + vecs[5]).astype(BF16)
    mean_term = jnp.mean(total, axis=-1, keepdims=True)
    proj_term = jnp.mean(total * own_unit, axis=-1, keepdims=True)
    input_grad = up_rows + own_inv * (total - mean_term - own_unit * proj_term)

    def columns(start, size):
        return jnp.swapaxes(reduced[:, :, start : start + size], 0, 1).reshape(rows, 2 * size)

    def columns_t(start, size):
        return jnp.swapaxes(reduced[:, :, start : start + size], 1, 2).reshape(2 * size, rows)

    off = sizes.small - sizes.tile
    fin = small_sum[1, :, off : off + 6].T
    qb_out = small_sum[0, :, off + 6 : off + 6 + sizes.qb_cols].reshape(-1)[: sizes.qkvb]
    ub_at = off + 6 + sizes.qb_cols
    ub_out = small_sum[0, :, ub_at : ub_at + sizes.ub_cols].reshape(-1)[: sizes.upb]
    return (
        hidden[None],
        input_grad,
        columns(sizes.qkv, qkv_q)[None],
        qb_out[None],
        columns_t(sizes.out, out_q)[None],
        fin[4][None],
        columns(0, up_q)[None],
        ub_out[None],
        columns_t(sizes.down, up_q)[None],
        fin[4][None],
        fin[0][None],
        fin[1][None],
        fin[2][None],
        fin[3][None],
    )


def solution(mesh):
    in_specs = (
        P(("dp", "tensor"), None),
        P("dp"),
        P("dp"),
        P(("dp", "tensor"), None),
        P(None, "dp", "tensor"),
        P(None, ("tensor", "dp")),
        P(None, "tensor", "dp"),
        P(None, "dp"),
        P(None, "dp", "tensor"),
        P(None, ("tensor", "dp")),
        P(None, "tensor", "dp"),
        P(None, "dp"),
        P(None, "dp"),
        P(None, "dp"),
        P(None, "dp"),
        P(None, "dp"),
    )
    out_specs = (
        P(None, ("dp", "tensor"), None),
        P(("dp", "tensor"), None),
        P(None, "dp", "tensor"),
        P(None, ("tensor", "dp")),
        P(None, "tensor", "dp"),
        P(None, "dp"),
        P(None, "dp", "tensor"),
        P(None, ("tensor", "dp")),
        P(None, "tensor", "dp"),
        P(None, "dp"),
        P(None, "dp"),
        P(None, "dp"),
        P(None, "dp"),
        P(None, "dp"),
    )
    return jax.shard_map(
        on_device, mesh=mesh, in_specs=in_specs, out_specs=out_specs, check_vma=False
    )
```
